256 devices in a mesh: ctx: 32 (over x, y, core), tp: 8 (over z).
Axes of the slice: x: 4, y: 4, z: 8, core: 2. Of those that a mesh axis runs over, the one named last changes fastest.
Arguments:
- queries: bfloat16 [49152, 4096], P('ctx', 'tp'), may hold values from -6 to 6
- keys: bfloat16 [49152, 4096], P('ctx', 'tp'), may hold values from -6 to 6
- values: bfloat16 [49152, 4096], P('ctx', 'tp'), may hold values from -51 to 51, as said below
- out_grad: bfloat16 [49152, 4096], P('ctx', 'tp'), may hold values from -6 to 6
- gain: float32 [4096], P('tp'), may hold values from 0.25 to 1.75
- doc_ids: int32 [192], P('ctx'), may hold values from 0 to 31, never falling along the last dimension, each value on 1 to 96 neighbouring positions
Outputs:
- normed: bfloat16 [49152, 4096], P('ctx', 'tp')
- query_grad: bfloat16 [49152, 4096], P('ctx', 'tp')
- key_grad: bfloat16 [49152, 4096], P('ctx', 'tp')
- value_grad: bfloat16 [49152, 4096], P('ctx', 'tp')
The draws below stay inside these ranges and needn't reach their ends.
Inputs may be any that keep to these rules, and one draw needn't show every extreme that they name: `doc_ids`: never falls along the sequence; each document covers 1 to max(4, 96) blocks, and one covers exactly that many. `values`: values of order one to ten, with scales that differ from token to token and from feature to feature.
All inputs are finite; a program needn't handle non-finite values.
Results may differ from the reference program's by a relative error of at most 0.0058.
Values sent between devices are 32-bit elements; how exact they have to be, the bound alone decides.
A program may use at most 128 MiB of HBM per device.

```python
import math
import jax
import jax.numpy as jnp
import numpy as np
from jax import lax

H = 32
HD = 128
C = 256
TOKENS = 49152
NCH = 192
QW = 4096


def draw_values(key, part):
    first_key, second_key, third_key = jax.random.split(key, 3)
    columns = jnp.arange(QW)
    head_index = (columns // HD).astype(jnp.float32)
    head_rise = head_index / max(H - 1, 1)
    noise_part = jnp.clip(jax.random.normal(first_key, (TOKENS, QW), jnp.float32), -4.0, 4.0)
    head_level = 3.0 ** (head_rise - 1.0)
    column_scale = jnp.exp(jax.random.uniform(second_key, (QW,), jnp.float32, 0.0, math.log(4.0)))
    row_scale = jnp.exp(jax.random.uniform(third_key, (TOKENS, 1), jnp.float32, -1.15, 1.15))
    return (noise_part * (head_level * column_scale)[None, :] * row_scale).astype(jnp.bfloat16)


def block_scale(key, extent, cuts, low, largest):
    loudness = 1.0
    for dim, parts in cuts:
        steps = jax.random.uniform(jax.random.fold_in(jax.random.fold_in(key, 6), dim), (parts,), jnp.float32, low / len(cuts), largest / len(cuts))
        loudness = loudness * jnp.repeat(jnp.exp(steps), extent[dim] // parts).reshape((-1,) + (1,) * (len(extent) - 1 - dim))
    return loudness


def length_profile(amount, total, bound, skew):
    weights = [(1 << 20) // math.isqrt(grade ** skew) + 1 for grade in range(2, amount + 1)]
    spare, counts = total - bound - (amount - 1), [1] * (amount - 1)
    while spare > 0:
        candidates = [i for i in range(amount - 1) if counts[i] < bound]
        mass, budget = sum([weights[i] for i in candidates]), spare
        for i in candidates:
            more = min(bound - counts[i], max(1, budget * weights[i] // mass), spare)
            counts[i] = counts[i] + more
            spare = spare - more
    return np.array([bound] + counts)


def uneven(own_key, number_of, total, bound, skew):
    if number_of == 2:
        one = jax.random.randint(own_key, (), max(1, total - bound), min(bound, total - 1) + 1)
        return jnp.stack([one, total - one])
    tallies = jnp.asarray(length_profile(number_of, total, bound, skew), jnp.int32)
    pairs = (number_of - 1) // 2
    giver, receiver = tallies[1:1 + 2 * pairs:2], tallies[2:2 + 2 * pairs:2]
    room = jnp.minimum(giver - 1, bound - receiver)
    shifted = jax.random.randint(jax.random.fold_in(own_key, 1), (pairs,), 0, 1 << 20) % (room + 1)
    tallies = tallies.at[1:1 + 2 * pairs:2].set(giver - shifted).at[2:2 + 2 * pairs:2].set(receiver + shifted)
    return tallies[jax.random.permutation(jax.random.fold_in(own_key, 2), number_of)]


def normal_values(stream_key, dims, spread, bound, shards=(), held_as=jnp.bfloat16):
    values = jax.random.normal(stream_key, dims, jnp.float32) * spread
    if len(shards) > 0:
        values = block_scale(stream_key, dims, shards, -0.22, 0.18) * values
    return jnp.clip(values, min=-bound, max=bound).astype(held_as)


def setup_inputs(seed: int = 0) -> dict:
    splits = jax.random.split(jax.random.key(seed), 7)
    return {
        "queries": normal_values(splits[0], (TOKENS, QW), 1.0, 6.0, ((0, 32), (1, 8))),
        "keys": normal_values(splits[1], (TOKENS, QW), 1.0, 6.0, ((0, 32), (1, 8))),
        "values": draw_values(jax.random.fold_in(splits[6], 71), 0),
        "out_grad": normal_values(splits[3], (TOKENS, QW), 1.0, 6.0, ((0, 32), (1, 8))),
        "gain": jnp.clip(1.0 + 0.15 * jax.random.normal(splits[4], (QW,), jnp.float32), 0.25, 1.75),
        "doc_ids": jnp.searchsorted(jnp.cumsum(uneven(splits[5], max(3, NCH // 6), NCH, max(4, NCH // 2), 1)), jnp.arange(NCH), side="right").astype(jnp.int32),
    }


epsilon = 1e-06

def to_low(array):
    return lax.optimization_barrier(array.astype(jnp.bfloat16)).astype(jnp.float32)

def reference(queries, keys, values, out_grad, gain, doc_ids):
    query_blk = queries.reshape(NCH, C, H, HD)
    key_blk = keys.reshape(NCH, C, H, HD)
    value_blk = values.reshape(NCH, C, H, HD)
    grad_blk = out_grad.reshape(NCH, C, QW)
    doc_of = doc_ids.astype(jnp.int32)
    earlier_doc = jnp.concatenate([jnp.full((1,), -1, jnp.int32), doc_of[:-1]])
    later_doc = jnp.concatenate([doc_of[1:], jnp.full((1,), -1, jnp.int32)])
    starts = doc_of != earlier_doc
    finals = doc_of != later_doc
    causal = jnp.tril(jnp.ones((C, C), dtype=bool))
    gain32 = gain.astype(jnp.float32)

    def forward(carried, pieces):
        query_c, key_c, value_c, grad_c, opens = pieces
        carried = jnp.where(opens, jnp.zeros_like(carried), carried)
        state_low = to_low(carried)
        query_f = query_c.astype(jnp.float32)
        key_f = key_c.astype(jnp.float32)
        value_f = value_c.astype(jnp.float32)
        scores = jnp.einsum('thd,shd->hts', query_f, key_f)
        scores = to_low(jnp.where(causal[None], scores, 0.0))
        attended = jnp.einsum('thd,hde->the', query_f, state_low) + jnp.einsum('hts,she->the', scores, value_f)
        flat_out = attended.reshape(C, QW)
        total_sq = lax.optimization_barrier(jnp.sum(flat_out * flat_out, axis=1, keepdims=True))
        scale_inv = lax.rsqrt(total_sq / QW + epsilon)
        normed = (flat_out * scale_inv * gain32).astype(jnp.bfloat16)
        weighted = grad_c.astype(jnp.float32) * gain32
        inner_sum = lax.optimization_barrier(jnp.sum(weighted * flat_out, axis=1, keepdims=True))
        mixed_grad = scale_inv * weighted - flat_out * scale_inv ** 3 * (inner_sum / QW)
        grad_low = mixed_grad.astype(jnp.bfloat16)
        grad_f = lax.optimization_barrier(grad_low).astype(jnp.float32).reshape(C, H, HD)
        grad_scores = to_low(jnp.where(causal[None], jnp.einsum('the,she->hts', grad_f, value_f), 0.0))
        query_grad = jnp.einsum('the,hde->thd', grad_f, state_low) + jnp.einsum('hts,shd->thd', grad_scores, key_f)
        carried = carried + jnp.einsum('shd,she->hde', key_f, value_f)
        return (carried, (normed, grad_low, query_grad.astype(jnp.bfloat16).reshape(C, QW)))
    start_state = jnp.zeros((H, HD, HD), jnp.float32)
    _, (normed, grad_low, query_grad) = lax.scan(forward, start_state, (query_blk, key_blk, value_blk, grad_blk, starts))

    def backward(carried, pieces):
        query_c, key_c, value_c, grad_c, closes = pieces
        carried = jnp.where(closes, jnp.zeros_like(carried), carried)
        state_low = to_low(carried)
        query_f = query_c.astype(jnp.float32)
        key_f = key_c.astype(jnp.float32)
        value_f = value_c.astype(jnp.float32)
        grad_f = grad_c.astype(jnp.float32).reshape(C, H, HD)
        scores = to_low(jnp.where(causal[None], jnp.einsum('thd,shd->hts', query_f, key_f), 0.0))
        grad_scores = to_low(jnp.where(causal[None], jnp.einsum('the,she->hts', grad_f, value_f), 0.0))
        key_grad = jnp.einsum('she,hde->shd', value_f, state_low) + jnp.einsum('hts,thd->shd', grad_scores, query_f)
        value_grad = jnp.einsum('shd,hde->she', key_f, state_low) + jnp.einsum('hts,the->she', scores, grad_f)
        carried = carried + jnp.einsum('thd,the->hde', query_f, grad_f)
        return (carried, (key_grad.astype(jnp.bfloat16).reshape(C, QW), value_grad.astype(jnp.bfloat16).reshape(C, QW)))
    _, (key_grad, value_grad) = lax.scan(backward, start_state, (query_blk, key_blk, value_blk, grad_low, finals), reverse=True)
    return (normed.reshape(TOKENS, QW), query_grad.reshape(TOKENS, QW), key_grad.reshape(TOKENS, QW), value_grad.reshape(TOKENS, QW))
```

```python
import functools

import jax
import jax.numpy as jnp
from jax import lax
from jax.experimental import pallas as pl
from jax.experimental.pallas import tpu as pltpu
from jax.sharding import PartitionSpec as P

HD = 128
C = 256
epsilon = 1e-06

MESH = pl.DeviceIdType.MESH
F32 = jnp.float32
BF16 = jnp.bfloat16


def mm(a, b, dims):
    return lax.dot_general(a, b, (dims, ((), ())), preferred_element_type=F32)


NN = ((1,), (0,))
NT = ((1,), (1,))
TN = ((0,), (0,))


def kernel(
    NC, NT_, NB, NH, QW,
    doc_ref, q_hbm, k_hbm, v_hbm, g_hbm, gain_ref,
    normed_hbm, qg_hbm, kg_hbm, vg_hbm,
    q_ref, k_ref, v_ref, g_ref,
    sc_ref, att_ref, d_ref, state_ref, enter_ref, leave_ref, kp_ref, vp_ref,
    o_norm, o_qg, o_kg, o_vg,
    docrow, docs,
    f_end, f_in, f_out, f_carry,
    b_end, b_in, b_out, b_carry,
    stat_send, stat_in,
    load_sem, store_sem, send_sem, doc_sem, f1_sem, f2_sem, b1_sem, b2_sem,
    tsend_sem, trecv_sem,
):
    PR = NH * HD // NC
    HP = HD // PR
    W = NH * HD
    me = lax.axis_index("ctx")
    mt = lax.axis_index("tp")

    def rows(n):
        return pl.ds(pl.multiple_of(n * C, C), C)

    def cols(h):
        return slice(h * HD, (h + 1) * HD)

    def load(i, hbm, ref, n):
        return pltpu.make_async_copy(hbm.at[rows(n)], ref.at[rows(n)], load_sem.at[i, n])

    loads = ((k_hbm, k_ref), (v_hbm, v_ref), (q_hbm, q_ref), (g_hbm, g_ref))

    barrier = pltpu.get_barrier_semaphore()

    @pl.loop(1, NC)
    def _(i):
        pl.semaphore_signal(
            barrier, inc=1, device_id={"ctx": lax.rem(me + i, NC)}, device_id_type=MESH
        )

    @pl.loop(1, NT_)
    def _(i):
        pl.semaphore_signal(
            barrier, inc=1, device_id={"tp": lax.rem(mt + i, NT_)}, device_id_type=MESH
        )

    @pl.loop(0, NB)
    def _(n):
        load(0, k_hbm, k_ref, n).start()
        load(1, v_hbm, v_ref, n).start()

    @pl.loop(0, NB)
    def _(n):
        load(2, q_hbm, q_ref, n).start()

    @pl.loop(0, NB)
    def _(n):
        load(3, g_hbm, g_ref, n).start()

    half = lax.broadcasted_iota(jnp.int32, (2, 128), 0)
    my_docs = jnp.where(half == 0, doc_ref[0], doc_ref[NB - 1]).astype(F32)
    docrow[...] = my_docs
    docs[me] = my_docs

    pl.semaphore_wait(barrier, NC - 1 + NT_ - 1)

    def exchange(i, src, dst, recv):
        return pltpu.make_async_remote_copy(
            src_ref=src,
            dst_ref=dst,
            send_sem=send_sem.at[i],
            recv_sem=recv.at[i],
            device_id={"ctx": lax.rem(me + i, NC)},
            device_id_type=MESH,
        )

    def doc_copy(i):
        return exchange(i, docrow, docs.at[me], doc_sem)

    @pl.loop(1, NC)
    def _(i):
        doc_copy(i).start()

    def f1_copy(i):
        return exchange(i, f_end.at[lax.rem(me + i, NC)], f_in.at[me], f1_sem)

    def f2_copy(i):
        return exchange(i, f_out.at[lax.rem(me + i, NC)], f_carry.at[me], f2_sem)

    def b1_copy(i):
        return exchange(i, b_end.at[lax.rem(me + i, NC)], b_in.at[me], b1_sem)

    def b2_copy(i):
        return exchange(i, b_out.at[lax.rem(me + i, NC)], b_carry.at[me], b2_sem)

    def start_all(copy):
        @pl.loop(1, NC)
        def _(i):
            copy(i).start()

    def wait_send(copy):
        @pl.loop(1, NC)
        def _(i):
            copy(i).wait_send()

    def wait_recv(copy):
        @pl.loop(1, NC)
        def _(i):
            copy(i).wait_recv()

    def same(a, b):
        return jnp.where(doc_ref[a] == doc_ref[b], 1.0, 0.0).astype(F32)

    def piece(h):
        return pl.ds(h * HP, HP)

    @pl.loop(0, NB)
    def _(n):
        load(0, k_hbm, k_ref, n).wait()
        load(1, v_hbm, v_ref, n).wait()
        prev = jnp.maximum(n - 1, 0)
        link = jnp.where(n > 0, same(prev, n), 0.0)
        for h in range(NH):
            kv = mm(k_ref[rows(n), cols(h)], v_ref[rows(n), cols(h)], TN).reshape(HP, PR, HD)
            run = jnp.where(link > 0.0, f_end[piece(h)], 0.0)
            state_ref[n, piece(h)] = run
            f_end[piece(h)] = run + kv

    wait_send(doc_copy)
    start_all(f1_copy)
    f_in[me] = f_end[me]

    causal = lax.broadcasted_iota(jnp.int32, (C, C), 0) >= lax.broadcasted_iota(
        jnp.int32, (C, C), 1
    )

    def inner(n):
        load(2, q_hbm, q_ref, n).wait()
        for h in range(NH):
            q = q_ref[rows(n), cols(h)]
            s = mm(q, k_ref[rows(n), cols(h)], NT)
            s = jnp.where(causal, s, 0.0).astype(BF16)
            sc_ref[n * NH + h] = s
            att_ref[rows(n), cols(h)] = mm(s, v_ref[rows(n), cols(h)], NN)

    @pl.loop(0, NB // 2)
    def _(n):
        inner(n)

    wait_recv(doc_copy)
    wait_recv(f1_copy)

    def fwd_step(j, run):
        before = jnp.maximum(j - 2, 0)
        last = docs[j - 1, 1:2, :]
        run = f_in[j - 1] + jnp.where((docs[before, 1:2, :] == last) & (j >= 2), run, 0.0)
        f_out[j] = jnp.where(last == docs[j, 0:1, :], run, 0.0)
        return run

    f_out[0] = jnp.zeros((PR, HD), F32)
    lax.fori_loop(1, NC, fwd_step, jnp.zeros((PR, HD), F32))
    wait_send(f1_copy)
    start_all(f2_copy)
    f_carry[me] = f_out[me]

    @pl.loop(NB // 2, NB)
    def _(n):
        inner(n)

    @pl.loop(0, NB)
    def _(n):
        load(3, g_hbm, g_ref, n).wait()

    wait_recv(f2_copy)

    gain = gain_ref[...]
    lane = lax.broadcasted_iota(jnp.int32, (C, 128), 1)
    stat = jnp.zeros((C, 128), F32)
    for n in range(NB):
        match = jnp.where(doc_ref[n] == doc_ref[0], 1.0, 0.0).astype(F32)
        sq = jnp.zeros((C, HD), F32)
        inn = jnp.zeros((C, HD), F32)
        for h in range(NH):
            enter = state_ref[n, piece(h)] + match * f_carry[piece(h)]
            enter = enter.reshape(HD, HD).astype(BF16)
            enter_ref[n, h] = enter
            att = att_ref[rows(n), cols(h)] + mm(q_ref[rows(n), cols(h)], enter, NN)
            att_ref[rows(n), cols(h)] = att
            sq = sq + att * att
            inn = inn + (g_ref[rows(n), cols(h)].astype(F32) * gain[:, cols(h)]) * att
        stat = jnp.where(lane == n, jnp.sum(sq, axis=1, keepdims=True), stat)
        stat = jnp.where(lane == 8 + n, jnp.sum(inn, axis=1, keepdims=True), stat)
    stat_t = jnp.transpose(stat)[0:16]
    stat_send[...] = stat_t
    stat_in[mt] = stat_t

    def t_copy(i):
        return pltpu.make_async_remote_copy(
            src_ref=stat_send,
            dst_ref=stat_in.at[mt],
            send_sem=tsend_sem.at[i],
            recv_sem=trecv_sem.at[i],
            device_id={"tp": lax.rem(mt + i, NT_)},
            device_id_type=MESH,
        )

    @pl.loop(1, NT_)
    def _(i):
        t_copy(i).start()

    wait_send(f2_copy)

    @pl.loop(1, NT_)
    def _(i):
        t_copy(i).wait()

    total = stat_in[0]
    for i in range(1, NT_):
        total = total + stat_in[i]
    r = lax.rsqrt(total[0:8] / QW + epsilon)
    coef = r * r * r * (total[8:16] / QW)
    packed = jnp.concatenate([r, coef, jnp.zeros((112, C), F32)], axis=0)
    columns = jnp.transpose(packed)

    for n in reversed(range(NB)):
        rc = columns[:, n : n + 1]
        cc = columns[:, 8 + n : 9 + n]
        for h in range(NH):
            att = att_ref[rows(n), cols(h)]
            w = g_ref[rows(n), cols(h)].astype(F32) * gain[:, cols(h)]
            d = (rc * w - att * cc).astype(BF16)
            d_ref[rows(n), cols(h)] = d
            o_norm[rows(n), cols(h)] = (att * rc * gain[:, cols(h)]).astype(BF16)
            qd = mm(q_ref[rows(n), cols(h)], d, TN).reshape(HP, PR, HD)
            if n == NB - 1:
                run = jnp.zeros((HP, PR, HD), F32)
            else:
                run = jnp.where(same(n, n + 1) > 0.0, b_end[piece(h)], 0.0)
            leave_ref[n, piece(h)] = run
            b_end[piece(h)] = run + qd

    start_all(b1_copy)
    b_in[me] = b_end[me]

    def store(i, ref, hbm, n):
        return pltpu.make_async_copy(ref.at[rows(n)], hbm.at[rows(n)], store_sem.at[i, n])

    def outer(n):
        store(0, o_norm, normed_hbm, n).start()
        for h in range(NH):
            q = q_ref[rows(n), cols(h)]
            d = d_ref[rows(n), cols(h)]
            gs = mm(d, v_ref[rows(n), cols(h)], NT)
            gs = jnp.where(causal, gs, 0.0).astype(BF16)
            qg = mm(d, enter_ref[n, h], NT) + mm(gs, k_ref[rows(n), cols(h)], NN)
            o_qg[rows(n), cols(h)] = qg.astype(BF16)
            kp_ref[rows(n), cols(h)] = mm(gs, q, TN)
            vp_ref[rows(n), cols(h)] = mm(sc_ref[n * NH + h], d, TN)
        store(1, o_qg, qg_hbm, n).start()

    @pl.loop(0, NB // 2)
    def _(n):
        outer(n)

    wait_recv(b1_copy)

    def bwd_step(t, run):
        j = NC - 1 - t
        after = jnp.minimum(j + 2, NC - 1)
        first = docs[j + 1, 0:1, :]
        run = b_in[j + 1] + jnp.where((docs[after, 0:1, :] == first) & (t >= 2), run, 0.0)
        b_out[j] = jnp.where(first == docs[j, 1:2, :], run, 0.0)
        return run

    b_out[NC - 1] = jnp.zeros((PR, HD), F32)
    lax.fori_loop(1, NC, bwd_step, jnp.zeros((PR, HD), F32))
    wait_send(b1_copy)
    start_all(b2_copy)
    b_carry[me] = b_out[me]

    @pl.loop(NB // 2, NB)
    def _(n):
        outer(n)

    wait_recv(b2_copy)

    @pl.loop(0, NB)
    def _(n):
        match = same(n, NB - 1)
        for h in range(NH):
            leave = leave_ref[n, piece(h)] + match * b_carry[piece(h)]
            leave = leave.reshape(HD, HD).astype(BF16)
            kg = kp_ref[rows(n), cols(h)] + mm(v_ref[rows(n), cols(h)], leave, NT)
            o_kg[rows(n), cols(h)] = kg.astype(BF16)
            vg = vp_ref[rows(n), cols(h)] + mm(k_ref[rows(n), cols(h)], leave, NN)
            o_vg[rows(n), cols(h)] = vg.astype(BF16)
        store(2, o_kg, kg_hbm, n).start()
        store(3, o_vg, vg_hbm, n).start()

    wait_send(b2_copy)

    @pl.loop(0, NB)
    def _(n):
        store(0, o_norm, normed_hbm, n).wait()
        store(1, o_qg, qg_hbm, n).wait()
        store(2, o_kg, kg_hbm, n).wait()
        store(3, o_vg, vg_hbm, n).wait()


def local(NC, NT_, queries, keys, values, out_grad, gain, doc_ids):
    tok, W = queries.shape
    NB, NH = tok // C, W // HD
    PR = NH * HD // NC
    QW = W * NT_
    any_spec = pl.BlockSpec(memory_space=pl.ANY)
    out = jax.ShapeDtypeStruct((tok, W), BF16)
    dma = pltpu.SemaphoreType.DMA
    ring = [pltpu.VMEM((NC, PR, HD), F32)] * 4
    return pl.pallas_call(
        functools.partial(kernel, NC, NT_, NB, NH, QW),
        out_shape=(out,) * 4,
        in_specs=[pl.BlockSpec(memory_space=pltpu.SMEM)]
        + [any_spec] * 4
        + [pl.BlockSpec(memory_space=pltpu.VMEM)],
        out_specs=(any_spec,) * 4,
        scratch_shapes=[pltpu.VMEM((tok, W), BF16)] * 4
        + [
            pltpu.VMEM((NB * NH, C, C), BF16),
            pltpu.VMEM((tok, W), F32),
            pltpu.VMEM((tok, W), BF16),
            pltpu.VMEM((NB, NC, PR, HD), F32),
            pltpu.VMEM((NB, NH, HD, HD), BF16),
            pltpu.VMEM((NB, NC, PR, HD), F32),
            pltpu.VMEM((tok, W), F32),
            pltpu.VMEM((tok, W), F32),
        ]
        + [pltpu.VMEM((tok, W), BF16)] * 4
        + [pltpu.VMEM((2, 128), F32), pltpu.VMEM((NC, 2, 128), F32)]
        + ring
        + ring
        + [
            pltpu.VMEM((16, C), F32),
            pltpu.VMEM((NT_, 16, C), F32),
            dma((4, NB)),
            dma((4, NB)),
            dma((NC,)),
            dma((NC,)),
            dma((NC,)),
            dma((NC,)),
            dma((NC,)),
            dma((NC,)),
            dma((NT_,)),
            dma((NT_,)),
        ],
        compiler_params=pltpu.CompilerParams(
            collective_id=0, has_side_effects=True, vmem_limit_bytes=60 * 2**20
        ),
        name="packed_linear_attention",
    )(doc_ids, queries, keys, values, out_grad, gain.reshape(1, W))


def solution(mesh):
    ctx, tp = mesh.shape["ctx"], mesh.shape["tp"]
    return jax.shard_map(
        functools.partial(local, ctx, tp),
        mesh=mesh,
        in_specs=(
            P("ctx", "tp"),
            P("ctx", "tp"),
            P("ctx", "tp"),
            P("ctx", "tp"),
            P("tp"),
            P("ctx"),
        ),
        out_specs=(P("ctx", "tp"), P("ctx", "tp"), P("ctx", "tp"), P("ctx", "tp")),
        check_vma=False,
    )
```

```python
import functools

import jax
import jax.numpy as jnp
from jax import lax
from jax.experimental import pallas as pl
from jax.experimental.pallas import tpu as pltpu
from jax.sharding import PartitionSpec as P

HD = 128
C = 256
epsilon = 1e-06

MESH = pl.DeviceIdType.MESH
F32 = jnp.float32
BF16 = jnp.bfloat16


def mm(a, b, dims):
    return lax.dot_general(a, b, (dims, ((), ())), preferred_element_type=F32)


NN = ((1,), (0,))
NT = ((1,), (1,))
TN = ((0,), (0,))


def kernel(
    NC, NT_, NB, NH, QW,
    doc_ref, q_hbm, k_hbm, v_hbm, g_hbm, gain_ref,
    o_norm, o_qg, kp_ref, vp_ref, low_ref, k_ref, v_ref,
    q_ref, g_ref,
    sc_ref, att_ref, d_ref, state_ref, enter_ref, leave_ref,
    docrow, docs,
    f_end, f_in, f_out, f_carry, f_swap, f_chip, f_give,
    b_end, b_in, b_out, b_carry, b_swap, b_chip, b_give,
    stat_send, stat_in,
    load_sem, send_sem, doc_sem, f1_sem, f2_sem, b1_sem, b2_sem,
    swap_send, swap_recv,
    tsend_sem, trecv_sem,
):
    PR = NH * HD // NC
    HP = HD // PR
    W = NH * HD
    NP = NC // 2
    HH = NH // 2
    me = lax.axis_index("ctx")
    mt = lax.axis_index("tp")
    core = lax.rem(me, 2)
    chip = me // 2
    other = 1 - core

    def rows(n):
        return pl.ds(pl.multiple_of(n * C, C), C)

    def cols(h):
        if isinstance(h, int):
            return slice(h * HD, (h + 1) * HD)
        return pl.ds(pl.multiple_of(h * HD, HD), HD)

    def load(i, hbm, ref, n):
        return pltpu.make_async_copy(hbm.at[rows(n)], ref.at[rows(n)], load_sem.at[i, n])

    loads = ((k_hbm, k_ref), (v_hbm, v_ref), (q_hbm, q_ref), (g_hbm, g_ref))

    barrier = pltpu.get_barrier_semaphore()

    @pl.loop(1, NC)
    def _(i):
        pl.semaphore_signal(
            barrier, inc=1, device_id={"ctx": lax.rem(me + i, NC)}, device_id_type=MESH
        )

    @pl.loop(1, NT_)
    def _(i):
        pl.semaphore_signal(
            barrier, inc=1, device_id={"tp": lax.rem(mt + i, NT_)}, device_id_type=MESH
        )

    @pl.loop(0, NB)
    def _(n):
        load(0, k_hbm, k_ref, n).start()
        load(1, v_hbm, v_ref, n).start()

    @pl.loop(0, NB)
    def _(n):
        load(2, q_hbm, q_ref, n).start()

    @pl.loop(0, NB)
    def _(n):
        load(3, g_hbm, g_ref, n).start()

    half = lax.broadcasted_iota(jnp.int32, (2, 128), 0)
    my_docs = jnp.where(half == 0, doc_ref[0], doc_ref[NB - 1]).astype(F32)
    docrow[...] = my_docs
    docs[me] = my_docs

    pl.semaphore_wait(barrier, NC - 1 + NT_ - 1)

    def exchange(i, src, dst, recv):
        return pltpu.make_async_remote_copy(
            src_ref=src,
            dst_ref=dst,
            send_sem=send_sem.at[i],
            recv_sem=recv.at[i],
            device_id={"ctx": lax.rem(me + i, NC)},
            device_id_type=MESH,
        )

    def doc_copy(i):
        return exchange(i, docrow, docs.at[me], doc_sem)

    @pl.loop(1, NC)
    def _(i):
        doc_copy(i).start()

    def chips(i, src, dst, recv):
        return pltpu.make_async_remote_copy(
            src_ref=src,
            dst_ref=dst,
            send_sem=send_sem.at[i],
            recv_sem=recv.at[i],
            device_id={"ctx": lax.rem(chip + i, NP) * 2 + core},
            device_id_type=MESH,
        )

    def f1_copy(i):
        return chips(i, f_chip.at[lax.rem(chip + i, NP)], f_in.at[chip], f1_sem)

    def f2_copy(i):
        return chips(i, f_out.at[lax.rem(chip + i, NP)], f_carry.at[core * NP + chip], f2_sem)

    def b1_copy(i):
        return chips(i, b_chip.at[lax.rem(chip + i, NP)], b_in.at[chip], b1_sem)

    def b2_copy(i):
        return chips(i, b_out.at[lax.rem(chip + i, NP)], b_carry.at[core * NP + chip], b2_sem)

    def swap(i, src, dst):
        return pltpu.make_async_remote_copy(
            src_ref=src,
            dst_ref=dst,
            send_sem=swap_send.at[i],
            recv_sem=swap_recv.at[i],
            device_id={"ctx": chip * 2 + other},
            device_id_type=MESH,
        )

    mine = pl.ds(core * NP, NP)
    theirs = pl.ds(other * NP, NP)
    f_swap_in = swap(0, f_end.at[theirs], f_swap)
    f_swap_out = swap(1, f_give, f_carry.at[mine])
    b_swap_in = swap(2, b_end.at[theirs], b_swap)
    b_swap_out = swap(3, b_give, b_carry.at[mine])

    def start_all(copy, count):
        @pl.loop(1, count)
        def _(i):
            copy(i).start()

    def wait_send(copy, count):
        @pl.loop(1, count)
        def _(i):
            copy(i).wait_send()

    def wait_recv(copy, count):
        @pl.loop(1, count)
        def _(i):
            copy(i).wait_recv()

    def same(a, b):
        return jnp.where(doc_ref[a] == doc_ref[b], 1.0, 0.0).astype(F32)

    def piece(h):
        return pl.ds(h * HP, HP)

    def states(n, first):
        prev = jnp.maximum(n - 1, 0)
        link = jnp.where(n > 0, same(prev, n), 0.0)
        for i in range(HH):
            h = first + i
            kv = mm(k_ref[rows(n), cols(h)], v_ref[rows(n), cols(h)], TN).reshape(HP, PR, HD)
            run = jnp.where(link > 0.0, f_end[piece(h)], 0.0)
            state_ref[n, piece(h)] = run
            f_end[piece(h)] = run + kv

    @pl.loop(0, NB)
    def _(n):
        load(0, k_hbm, k_ref, n).wait()
        load(1, v_hbm, v_ref, n).wait()
        states(n, other * HH)

    f_swap_in.start()

    @pl.loop(0, NB)
    def _(n):
        states(n, core * HH)

    wait_send(doc_copy, NC)
    wait_recv(doc_copy, NC)
    first0, last0 = docs[chip * 2, 0:1, :], docs[chip * 2, 1:2, :]
    first1, last1 = docs[chip * 2 + 1, 0:1, :], docs[chip * 2 + 1, 1:2, :]
    is0 = core == 0

    def choose(cond, x):
        return jnp.where(cond, x, 0.0)

    f_swap_in.wait_recv()

    @pl.loop(0, NP)
    def _(i):
        own, got = f_end[core * NP + i], f_swap[i]
        e0, e1 = jnp.where(is0, own, got), jnp.where(is0, got, own)
        f_chip[i] = e1 + choose(last0 == last1, e0)

    start_all(f1_copy, NP)
    f_in[chip] = f_chip[chip]

    causal = lax.broadcasted_iota(jnp.int32, (C, C), 0) >= lax.broadcasted_iota(
        jnp.int32, (C, C), 1
    )

    def inner(n):
        load(2, q_hbm, q_ref, n).wait()
        for h in range(NH):
            q = q_ref[rows(n), cols(h)]
            s = mm(q, k_ref[rows(n), cols(h)], NT)
            s = jnp.where(causal, s, 0.0).astype(BF16)
            sc_ref[n * NH + h] = s
            att_ref[rows(n), cols(h)] = mm(s, v_ref[rows(n), cols(h)], NN)

    @pl.loop(0, NB // 2)
    def _(n):
        inner(n)

    wait_recv(f1_copy, NP)

    def fwd_step(j, run):
        before = jnp.maximum(j - 2, 0)
        last = docs[2 * j - 1, 1:2, :]
        run = f_in[j - 1] + choose((docs[2 * before + 1, 1:2, :] == last) & (j >= 2), run)
        f_out[j] = choose(last == docs[2 * j, 0:1, :], run)
        return run

    f_out[0] = jnp.zeros((PR, HD), F32)
    lax.fori_loop(1, NP, fwd_step, jnp.zeros((PR, HD), F32))
    wait_send(f1_copy, NP)
    start_all(f2_copy, NP)
    f_carry[core * NP + chip] = f_out[chip]

    @pl.loop(NB // 2, NB)
    def _(n):
        inner(n)

    @pl.loop(0, NB)
    def _(n):
        load(3, g_hbm, g_ref, n).wait()

    wait_recv(f2_copy, NP)

    @pl.loop(0, NP)
    def _(i):
        x = f_carry[core * NP + i]
        e0 = jnp.where(is0, f_end[core * NP + i], f_swap[i])
        second = choose(last0 == first1, e0) + choose(first0 == first1, x)
        f_give[i] = jnp.where(is0, second, x)
        f_carry[core * NP + i] = jnp.where(is0, x, second)

    f_swap_out.start()
    f_swap_out.wait_recv()

    gain = gain_ref[...]
    lane = lax.broadcasted_iota(jnp.int32, (C, 128), 1)
    stat = jnp.zeros((C, 128), F32)
    for n in range(NB):
        match = jnp.where(doc_ref[n] == doc_ref[0], 1.0, 0.0).astype(F32)
        sq = jnp.zeros((C, HD), F32)
        inn = jnp.zeros((C, HD), F32)
        for h in range(NH):
            enter = state_ref[n, piece(h)] + match * f_carry[piece(h)]
            enter = enter.reshape(HD, HD).astype(BF16)
            enter_ref[n, h] = enter
            att = att_ref[rows(n), cols(h)] + mm(q_ref[rows(n), cols(h)], enter, NN)
            att_ref[rows(n), cols(h)] = att
            sq = sq + att * att
            inn = inn + (g_ref[rows(n), cols(h)].astype(F32) * gain[:, cols(h)]) * att
        stat = jnp.where(lane == n, jnp.sum(sq, axis=1, keepdims=True), stat)
        stat = jnp.where(lane == 8 + n, jnp.sum(inn, axis=1, keepdims=True), stat)
    stat_t = jnp.transpose(stat)[0:16]
    stat_send[...] = stat_t
    stat_in[mt] = stat_t

    def t_copy(i):
        return pltpu.make_async_remote_copy(
            src_ref=stat_send,
            dst_ref=stat_in.at[mt],
            send_sem=tsend_sem.at[i],
            recv_sem=trecv_sem.at[i],
            device_id={"tp": lax.rem(mt + i, NT_)},
            device_id_type=MESH,
        )

    @pl.loop(1, NT_)
    def _(i):
        t_copy(i).start()

    wait_send(f2_copy, NP)

    @pl.loop(1, NT_)
    def _(i):
        t_copy(i).wait()

    total = stat_in[0]
    for i in range(1, NT_):
        total = total + stat_in[i]
    r = lax.rsqrt(total[0:8] / QW + epsilon)
    coef = r * r * r * (total[8:16] / QW)
    packed = jnp.concatenate([r, coef, jnp.zeros((112, C), F32)], axis=0)
    columns = jnp.transpose(packed)

    def back(first):
        for n in reversed(range(NB)):
            rc = columns[:, n : n + 1]
            cc = columns[:, 8 + n : 9 + n]
            for i in range(HH):
                h = first + i
                att = att_ref[rows(n), cols(h)]
                w = g_ref[rows(n), cols(h)].astype(F32) * gain_ref[:, cols(h)]
                d = (rc * w - att * cc).astype(BF16)
                d_ref[rows(n), cols(h)] = d
                o_norm[rows(n), cols(h)] = (att * rc * gain_ref[:, cols(h)]).astype(BF16)
                qd = mm(q_ref[rows(n), cols(h)], d, TN).reshape(HP, PR, HD)
                if n == NB - 1:
                    run = jnp.zeros((HP, PR, HD), F32)
                else:
                    run = jnp.where(same(n, n + 1) > 0.0, b_end[piece(h)], 0.0)
                leave_ref[n, piece(h)] = run
                b_end[piece(h)] = run + qd

    back(other * HH)
    b_swap_in.start()
    back(core * HH)
    b_swap_in.wait_recv()

    @pl.loop(0, NP)
    def _(i):
        own, got = b_end[core * NP + i], b_swap[i]
        e0, e1 = jnp.where(is0, own, got), jnp.where(is0, got, own)
        b_chip[i] = e0 + choose(first0 == first1, e1)

    start_all(b1_copy, NP)
    b_in[chip] = b_chip[chip]

    def outer(n):
        for h in range(NH):
            q = q_ref[rows(n), cols(h)]
            d = d_ref[rows(n), cols(h)]
            gs = mm(d, v_ref[rows(n), cols(h)], NT)
            gs = jnp.where(causal, gs, 0.0).astype(BF16)
            qg = mm(d, enter_ref[n, h], NT) + mm(gs, k_ref[rows(n), cols(h)], NN)
            o_qg[rows(n), cols(h)] = qg.astype(BF16)
            kp_ref[rows(n), cols(h)] = mm(gs, q, TN)
            vp_ref[rows(n), cols(h)] = mm(sc_ref[n * NH + h], d, TN)

    @pl.loop(0, NB // 2)
    def _(n):
        outer(n)

    wait_recv(b1_copy, NP)

    def bwd_step(t, run):
        j = NP - 1 - t
        after = jnp.minimum(j + 2, NP - 1)
        first = docs[2 * j + 2, 0:1, :]
        run = b_in[j + 1] + choose((docs[2 * after, 0:1, :] == first) & (t >= 2), run)
        b_out[j] = choose(first == docs[2 * j + 1, 1:2, :], run)
        return run

    b_out[NP - 1] = jnp.zeros((PR, HD), F32)
    lax.fori_loop(1, NP, bwd_step, jnp.zeros((PR, HD), F32))
    wait_send(b1_copy, NP)
    start_all(b2_copy, NP)
    b_carry[core * NP + chip] = b_out[chip]

    @pl.loop(NB // 2, NB)
    def _(n):
        outer(n)

    wait_recv(b2_copy, NP)

    @pl.loop(0, NP)
    def _(i):
        x = b_carry[core * NP + i]
        e1 = jnp.where(is0, b_swap[i], b_end[core * NP + i])
        second = choose(first1 == last0, e1) + choose(last1 == last0, x)
        b_give[i] = jnp.where(is0, x, second)
        b_carry[core * NP + i] = jnp.where(is0, second, x)

    b_swap_out.start()
    b_swap_out.wait_recv()

    @pl.loop(0, NB)
    def _(n):
        match = same(n, NB - 1)
        for h in range(NH):
            leave = leave_ref[n, piece(h)] + match * b_carry[piece(h)]
            low_ref[n, h] = leave.reshape(HD, HD).astype(BF16)

    wait_send(b2_copy, NP)
    for copy in (f_swap_in, f_swap_out, b_swap_in, b_swap_out):
        copy.wait_send()


def finish(
    NB, NH,
    norm_ref, qg_ref, kp_ref, vp_ref, low_ref, k_ref, v_ref,
    normed_hbm, qg_hbm, kg_hbm, vg_hbm,
    o_kg, o_vg, store_sem,
):
    def rows(n):
        return pl.ds(pl.multiple_of(n * C, C), C)

    def store(i, ref, hbm, n):
        return pltpu.make_async_copy(ref.at[rows(n)], hbm.at[rows(n)], store_sem.at[i, n])

    @pl.loop(0, NB)
    def _(n):
        store(0, norm_ref, normed_hbm, n).start()
        store(1, qg_ref, qg_hbm, n).start()

    @pl.loop(0, NB)
    def _(n):
        for h in range(NH):
            at = slice(h * HD, (h + 1) * HD)
            leave = low_ref[n, h]
            kg = kp_ref[rows(n), at] + mm(v_ref[rows(n), at], leave, NT)
            o_kg[rows(n), at] = kg.astype(BF16)
            vg = vp_ref[rows(n), at] + mm(k_ref[rows(n), at], leave, NN)
            o_vg[rows(n), at] = vg.astype(BF16)
        store(2, o_kg, kg_hbm, n).start()
        store(3, o_vg, vg_hbm, n).start()

    @pl.loop(0, NB)
    def _(n):
        store(0, norm_ref, normed_hbm, n).wait()
        store(1, qg_ref, qg_hbm, n).wait()
        store(2, o_kg, kg_hbm, n).wait()
        store(3, o_vg, vg_hbm, n).wait()


def local(NC, NT_, queries, keys, values, out_grad, gain, doc_ids):
    tok, W = queries.shape
    NB, NH = tok // C, W // HD
    PR = NH * HD // NC
    QW = W * NT_
    any_spec = pl.BlockSpec(memory_space=pl.ANY)
    vmem_spec = pl.BlockSpec(memory_space=pltpu.VMEM)
    out = jax.ShapeDtypeStruct((tok, W), BF16)
    dma = pltpu.SemaphoreType.DMA
    whole = pltpu.VMEM((NC, PR, HD), F32)
    part = pltpu.VMEM((NC // 2, PR, HD), F32)
    ring = [whole, part, part, whole, part, part, part]
    held = (
        pltpu.VMEM((tok, W), BF16),
        pltpu.VMEM((tok, W), BF16),
        pltpu.VMEM((tok, W), F32),
        pltpu.VMEM((tok, W), F32),
        pltpu.VMEM((NB, NH, HD, HD), BF16),
        pltpu.VMEM((tok, W), BF16),
        pltpu.VMEM((tok, W), BF16),
    )
    inner = pl.pallas_call(
        functools.partial(kernel, NC, NT_, NB, NH, QW),
        out_shape=held,
        in_specs=[pl.BlockSpec(memory_space=pltpu.SMEM)] + [any_spec] * 4 + [vmem_spec],
        out_specs=(vmem_spec,) * 7,
        scratch_shapes=[pltpu.VMEM((tok, W), BF16)] * 2
        + [
            pltpu.VMEM((NB * NH, C, C), BF16),
            pltpu.VMEM((tok, W), F32),
            pltpu.VMEM((tok, W), BF16),
            pltpu.VMEM((NB, NC, PR, HD), F32),
            pltpu.VMEM((NB, NH, HD, HD), BF16),
            pltpu.VMEM((NB, NC, PR, HD), F32),
        ]
        + [pltpu.VMEM((2, 128), F32), pltpu.VMEM((NC, 2, 128), F32)]
        + ring
        + ring
        + [
            pltpu.VMEM((16, C), F32),
            pltpu.VMEM((NT_, 16, C), F32),
            dma((4, NB)),
            dma((NC,)),
            dma((NC,)),
            dma((NC // 2,)),
            dma((NC // 2,)),
            dma((NC // 2,)),
            dma((NC // 2,)),
            dma((4,)),
            dma((4,)),
            dma((NT_,)),
            dma((NT_,)),
        ],
        compiler_params=pltpu.CompilerParams(
            collective_id=0, has_side_effects=True, vmem_limit_bytes=47 * 2**20
        ),
        name="packed_linear_attention",
    )(doc_ids, queries, keys, values, out_grad, gain.reshape(1, W))
    return pl.pallas_call(
        functools.partial(finish, NB, NH),
        out_shape=(out,) * 4,
        in_specs=[vmem_spec] * 7,
        out_specs=(any_spec,) * 4,
        scratch_shapes=[pltpu.VMEM((tok, W), BF16)] * 2 + [dma((4, NB))],
        compiler_params=pltpu.CompilerParams(vmem_limit_bytes=8 * 2**20),
        name="key_value_grads",
    )(*inner)


def solution(mesh):
    ctx, tp = mesh.shape["ctx"], mesh.shape["tp"]
    return jax.shard_map(
        functools.partial(local, ctx, tp),
        mesh=mesh,
        in_specs=(
            P("ctx", "tp"),
            P("ctx", "tp"),
            P("ctx", "tp"),
            P("ctx", "tp"),
            P("tp"),
            P("ctx"),
        ),
        out_specs=(P("ctx", "tp"), P("ctx", "tp"), P("ctx", "tp"), P("ctx", "tp")),
        check_vma=False,
    )
```

```python
import functools
import math

import jax
import jax.numpy as jnp
from jax import lax
from jax.experimental import pallas as pl
from jax.experimental.pallas import tpu as pltpu
from jax.sharding import PartitionSpec as P

HD = 128
C = 256
epsilon = 1e-06

MESH = pl.DeviceIdType.MESH
F32 = jnp.float32
BF16 = jnp.bfloat16


def mm(a, b, dims):
    return lax.dot_general(a, b, (dims, ((), ())), preferred_element_type=F32)


NN = ((1,), (0,))
NT = ((1,), (1,))
TN = ((0,), (0,))


def kernel(
    NC, NT_, NB, NH, QW,
    doc_ref, q_hbm, k_hbm, v_hbm, g_hbm, gain_ref,
    o_norm, o_qg, kp_ref, vp_ref, low_ref, k_ref, v_ref,
    q_ref, g_ref,
    sc_ref, att_ref, d_ref, state_ref, enter_ref, leave_ref,
    sq_ref, inn_ref, docrow, docs,
    f_end, f_in, f_out, f_carry, f_swap, f_chip, f_give,
    b_end, b_in, b_out, b_carry, b_swap, b_chip, b_give,
    stat_send, stat_in,
    load_sem, send_sem, doc_sem, f1_sem, f2_sem, b1_sem, b2_sem,
    swap_send, swap_recv,
    tsend_sem, trecv_sem,
):
    PR = NH * HD // NC
    HP = HD // PR
    W = NH * HD
    NP = NC // 2
    HH = NH // 2
    me = lax.axis_index("ctx")
    mt = lax.axis_index("tp")
    core = lax.rem(me, 2)
    chip = me // 2
    other = 1 - core

    def rows(n):
        return pl.ds(pl.multiple_of(n * C, C), C)

    def cols(h):
        if isinstance(h, int):
            return slice(h * HD, (h + 1) * HD)
        return pl.ds(pl.multiple_of(h * HD, HD), HD)

    def load(i, hbm, ref, n):
        return pltpu.make_async_copy(hbm.at[rows(n)], ref.at[rows(n)], load_sem.at[i, n])

    loads = ((k_hbm, k_ref), (v_hbm, v_ref), (q_hbm, q_ref), (g_hbm, g_ref))

    barrier = pltpu.get_barrier_semaphore()

    @pl.loop(1, NC)
    def _(i):
        pl.semaphore_signal(
            barrier, inc=1, device_id={"ctx": lax.rem(me + i, NC)}, device_id_type=MESH
        )

    @pl.loop(1, NT_)
    def _(i):
        pl.semaphore_signal(
            barrier, inc=1, device_id={"tp": lax.rem(mt + i, NT_)}, device_id_type=MESH
        )

    @pl.loop(0, NB)
    def _(n):
        load(0, k_hbm, k_ref, n).start()
        load(1, v_hbm, v_ref, n).start()

    @pl.loop(0, NB)
    def _(n):
        load(2, q_hbm, q_ref, n).start()

    @pl.loop(0, NB)
    def _(n):
        load(3, g_hbm, g_ref, n).start()

    half = lax.broadcasted_iota(jnp.int32, (2, 128), 0)
    my_docs = jnp.where(half == 0, doc_ref[0], doc_ref[NB - 1]).astype(F32)
    docrow[...] = my_docs
    docs[me] = my_docs

    pl.semaphore_wait(barrier, NC - 1 + NT_ - 1)

    def exchange(i, src, dst, recv):
        return pltpu.make_async_remote_copy(
            src_ref=src,
            dst_ref=dst,
            send_sem=send_sem.at[i],
            recv_sem=recv.at[i],
            device_id={"ctx": lax.rem(me + i, NC)},
            device_id_type=MESH,
        )

    def doc_copy(i):
        return exchange(i, docrow, docs.at[me], doc_sem)

    @pl.loop(1, NC)
    def _(i):
        doc_copy(i).start()

    side = math.isqrt(NP)
    if side * side != NP:
        side = 1

    def to(i):
        row = lax.rem(chip // side + i // side, NP // side)
        return row * side + lax.rem(chip + i, side)

    def far(n, i):
        return min(i, n - i)

    order = sorted(
        range(1, NP), key=lambda i: -far(NP // side, i // side) - far(side, i % side)
    )

    def chips(i, src, dst, recv):
        return pltpu.make_async_remote_copy(
            src_ref=src,
            dst_ref=dst,
            send_sem=send_sem.at[i],
            recv_sem=recv.at[i],
            device_id={"ctx": to(i) * 2 + core},
            device_id_type=MESH,
        )

    def f1_copy(i):
        return chips(i, f_chip.at[to(i)], f_in.at[chip], f1_sem)

    def f2_copy(i):
        return chips(i, f_out.at[to(i)], f_carry.at[core * NP + chip], f2_sem)

    def b1_copy(i):
        return chips(i, b_chip.at[to(i)], b_in.at[chip], b1_sem)

    def b2_copy(i):
        return chips(i, b_out.at[to(i)], b_carry.at[core * NP + chip], b2_sem)

    def swap(i, src, dst):
        return pltpu.make_async_remote_copy(
            src_ref=src,
            dst_ref=dst,
            send_sem=swap_send.at[i],
            recv_sem=swap_recv.at[i],
            device_id={"ctx": chip * 2 + other},
            device_id_type=MESH,
        )

    mine = pl.ds(core * NP, NP)
    theirs = pl.ds(other * NP, NP)
    f_swap_in = swap(0, f_end.at[theirs], f_swap)
    f_swap_out = swap(1, f_give, f_carry.at[mine])
    b_swap_in = swap(2, b_end.at[theirs], b_swap)
    b_swap_out = swap(3, b_give, b_carry.at[mine])

    def start_all(copy, count):
        @pl.loop(1, count)
        def _(i):
            copy(i).start()

    def start_far(copy):
        for i in order:
            copy(i).start()

    def wait_send(copy, count):
        @pl.loop(1, count)
        def _(i):
            copy(i).wait_send()

    def wait_recv(copy, count):
        @pl.loop(1, count)
        def _(i):
            copy(i).wait_recv()

    def same(a, b):
        return jnp.where(doc_ref[a] == doc_ref[b], 1.0, 0.0).astype(F32)

    def piece(h):
        return pl.ds(h * HP, HP)

    def states(n, first):
        prev = jnp.maximum(n - 1, 0)
        link = jnp.where(n > 0, same(prev, n), 0.0)
        for i in range(HH):
            h = first + i
            kv = mm(k_ref[rows(n), cols(h)], v_ref[rows(n), cols(h)], TN).reshape(HP, PR, HD)
            run = jnp.where(link > 0.0, f_end[piece(h)], 0.0)
            state_ref[n, piece(h)] = run
            f_end[piece(h)] = run + kv

    @pl.loop(0, NB)
    def _(n):
        load(0, k_hbm, k_ref, n).wait()
        load(1, v_hbm, v_ref, n).wait()
        states(n, other * HH)

    f_swap_in.start()

    @pl.loop(0, NB)
    def _(n):
        states(n, core * HH)

    wait_send(doc_copy, NC)
    wait_recv(doc_copy, NC)
    first0, last0 = docs[chip * 2, 0:1, :], docs[chip * 2, 1:2, :]
    first1, last1 = docs[chip * 2 + 1, 0:1, :], docs[chip * 2 + 1, 1:2, :]
    is0 = core == 0

    def choose(cond, x):
        return jnp.where(cond, x, 0.0)

    f_swap_in.wait_recv()

    own, got = f_end[mine], f_swap[...]
    e0, e1 = jnp.where(is0, own, got), jnp.where(is0, got, own)
    f_chip[...] = e1 + choose((last0 == last1)[None], e0)

    start_far(f1_copy)
    f_in[chip] = f_chip[chip]

    causal = lax.broadcasted_iota(jnp.int32, (C, C), 0) >= lax.broadcasted_iota(
        jnp.int32, (C, C), 1
    )

    def inner(n):
        load(2, q_hbm, q_ref, n).wait()
        for h in range(NH):
            q = q_ref[rows(n), cols(h)]
            s = mm(q, k_ref[rows(n), cols(h)], NT)
            s = jnp.where(causal, s, 0.0).astype(BF16)
            sc_ref[n * NH + h] = s
            att_ref[rows(n), cols(h)] = mm(s, v_ref[rows(n), cols(h)], NN)

    @pl.loop(0, NB // 2)
    def _(n):
        inner(n)

    wait_recv(f1_copy, NP)

    def fwd_step(j, run):
        before = jnp.maximum(j - 2, 0)
        last = docs[2 * j - 1, 1:2, :]
        run = f_in[j - 1] + choose((docs[2 * before + 1, 1:2, :] == last) & (j >= 2), run)
        f_out[j] = choose(last == docs[2 * j, 0:1, :], run)
        return run

    f_out[0] = jnp.zeros((PR, HD), F32)
    lax.fori_loop(1, NP, fwd_step, jnp.zeros((PR, HD), F32), unroll=True)
    wait_send(f1_copy, NP)
    start_far(f2_copy)
    f_carry[core * NP + chip] = f_out[chip]

    @pl.loop(NB // 2, NB)
    def _(n):
        inner(n)

    @pl.loop(0, NB)
    def _(n):
        load(3, g_hbm, g_ref, n).wait()

    wait_recv(f2_copy, NP)

    x = f_carry[mine]
    e0 = jnp.where(is0, f_end[mine], f_swap[...])
    second = choose((last0 == first1)[None], e0) + choose((first0 == first1)[None], x)
    f_give[...] = jnp.where(is0, second, x)
    f_swap_out.start()
    f_carry[mine] = jnp.where(is0, x, second)

    lane = lax.broadcasted_iota(jnp.int32, (C, 128), 1)
    def attend(n, first, sq, inn):
        match = jnp.where(doc_ref[n] == doc_ref[0], 1.0, 0.0).astype(F32)
        for i in range(HH):
            h = first + i
            enter = state_ref[n, piece(h)] + match * f_carry[piece(h)]
            enter = enter.reshape(HD, HD).astype(BF16)
            enter_ref[n, h] = enter
            att = att_ref[rows(n), cols(h)] + mm(q_ref[rows(n), cols(h)], enter, NN)
            att_ref[rows(n), cols(h)] = att
            sq = sq + att * att
            inn = inn + (g_ref[rows(n), cols(h)].astype(F32) * gain_ref[:, cols(h)]) * att
        return sq, inn

    for n in range(NB):
        zero = jnp.zeros((C, HD), F32)
        sq_ref[rows(n)], inn_ref[rows(n)] = attend(n, core * HH, zero, zero)
    f_swap_out.wait_recv()
    stat = jnp.zeros((C, 128), F32)
    for n in range(NB):
        sq, inn = attend(n, other * HH, sq_ref[rows(n)], inn_ref[rows(n)])
        stat = jnp.where(lane == n, jnp.sum(sq, axis=1, keepdims=True), stat)
        stat = jnp.where(lane == 8 + n, jnp.sum(inn, axis=1, keepdims=True), stat)
    stat_t = jnp.transpose(stat)[0:16]
    stat_send[...] = stat_t
    stat_in[mt] = stat_t

    def t_copy(i):
        return pltpu.make_async_remote_copy(
            src_ref=stat_send,
            dst_ref=stat_in.at[mt],
            send_sem=tsend_sem.at[i],
            recv_sem=trecv_sem.at[i],
            device_id={"tp": lax.rem(mt + i, NT_)},
            device_id_type=MESH,
        )

    @pl.loop(1, NT_)
    def _(i):
        t_copy(i).start()

    wait_send(f2_copy, NP)

    @pl.loop(1, NT_)
    def _(i):
        t_copy(i).wait()

    total = stat_in[0]
    for i in range(1, NT_):
        total = total + stat_in[i]
    r = lax.rsqrt(total[0:8] / QW + epsilon)
    coef = r * r * r * (total[8:16] / QW)
    packed = jnp.concatenate([r, coef, jnp.zeros((112, C), F32)], axis=0)
    columns = jnp.transpose(packed)

    def back(first):
        for n in reversed(range(NB)):
            rc = columns[:, n : n + 1]
            cc = columns[:, 8 + n : 9 + n]
            for i in range(HH):
                h = first + i
                att = att_ref[rows(n), cols(h)]
                w = g_ref[rows(n), cols(h)].astype(F32) * gain_ref[:, cols(h)]
                d = (rc * w - att * cc).astype(BF16)
                d_ref[rows(n), cols(h)] = d
                o_norm[rows(n), cols(h)] = (att * rc * gain_ref[:, cols(h)]).astype(BF16)
                qd = mm(q_ref[rows(n), cols(h)], d, TN).reshape(HP, PR, HD)
                if n == NB - 1:
                    run = jnp.zeros((HP, PR, HD), F32)
                else:
                    run = jnp.where(same(n, n + 1) > 0.0, b_end[piece(h)], 0.0)
                leave_ref[n, piece(h)] = run
                b_end[piece(h)] = run + qd

    back(other * HH)
    b_swap_in.start()
    back(core * HH)
    b_swap_in.wait_recv()

    own, got = b_end[mine], b_swap[...]
    e0, e1 = jnp.where(is0, own, got), jnp.where(is0, got, own)
    b_chip[...] = e0 + choose((first0 == first1)[None], e1)

    start_far(b1_copy)
    b_in[chip] = b_chip[chip]

    def outer(n):
        for h in range(NH):
            q = q_ref[rows(n), cols(h)]
            d = d_ref[rows(n), cols(h)]
            gs = mm(d, v_ref[rows(n), cols(h)], NT)
            gs = jnp.where(causal, gs, 0.0).astype(BF16)
            qg = mm(d, enter_ref[n, h], NT) + mm(gs, k_ref[rows(n), cols(h)], NN)
            o_qg[rows(n), cols(h)] = qg.astype(BF16)
            kp_ref[rows(n), cols(h)] = mm(gs, q, TN)
            vp_ref[rows(n), cols(h)] = mm(sc_ref[n * NH + h], d, TN)

    @pl.loop(0, NB // 2)
    def _(n):
        outer(n)

    wait_recv(b1_copy, NP)

    def bwd_step(t, run):
        j = NP - 1 - t
        after = jnp.minimum(j + 2, NP - 1)
        first = docs[2 * j + 2, 0:1, :]
        run = b_in[j + 1] + choose((docs[2 * after, 0:1, :] == first) & (t >= 2), run)
        b_out[j] = choose(first == docs[2 * j + 1, 1:2, :], run)
        return run

    b_out[NP - 1] = jnp.zeros((PR, HD), F32)
    lax.fori_loop(1, NP, bwd_step, jnp.zeros((PR, HD), F32), unroll=True)
    wait_send(b1_copy, NP)
    start_far(b2_copy)
    b_carry[core * NP + chip] = b_out[chip]

    @pl.loop(NB // 2, NB)
    def _(n):
        outer(n)

    wait_recv(b2_copy, NP)

    x = b_carry[mine]
    e1 = jnp.where(is0, b_swap[...], b_end[mine])
    second = choose((first1 == last0)[None], e1) + choose((last1 == last0)[None], x)
    b_give[...] = jnp.where(is0, x, second)
    b_swap_out.start()
    b_carry[mine] = jnp.where(is0, second, x)

    def lower(first):
        for n in range(NB):
            match = same(n, NB - 1)
            for i in range(HH):
                h = first + i
                leave = leave_ref[n, piece(h)] + match * b_carry[piece(h)]
                low_ref[n, h] = leave.reshape(HD, HD).astype(BF16)

    lower(core * HH)
    b_swap_out.wait_recv()
    lower(other * HH)

    wait_send(b2_copy, NP)
    for copy in (f_swap_in, f_swap_out, b_swap_in, b_swap_out):
        copy.wait_send()


def finish(
    NB, NH,
    norm_ref, qg_ref, kp_ref, vp_ref, low_ref, k_ref, v_ref,
    normed_hbm, qg_hbm, kg_hbm, vg_hbm,
    o_kg, o_vg, store_sem,
):
    def rows(n):
        return pl.ds(pl.multiple_of(n * C, C), C)

    def store(i, ref, hbm, n):
        return pltpu.make_async_copy(ref.at[rows(n)], hbm.at[rows(n)], store_sem.at[i, n])

    @pl.loop(0, NB)
    def _(n):
        store(0, norm_ref, normed_hbm, n).start()
        store(1, qg_ref, qg_hbm, n).start()

    @pl.loop(0, NB)
    def _(n):
        for h in range(NH):
            at = slice(h * HD, (h + 1) * HD)
            leave = low_ref[n, h]
            kg = kp_ref[rows(n), at] + mm(v_ref[rows(n), at], leave, NT)
            o_kg[rows(n), at] = kg.astype(BF16)
            vg = vp_ref[rows(n), at] + mm(k_ref[rows(n), at], leave, NN)
            o_vg[rows(n), at] = vg.astype(BF16)
        store(2, o_kg, kg_hbm, n).start()
        store(3, o_vg, vg_hbm, n).start()

    @pl.loop(0, NB)
    def _(n):
        store(0, norm_ref, normed_hbm, n).wait()
        store(1, qg_ref, qg_hbm, n).wait()
        store(2, o_kg, kg_hbm, n).wait()
        store(3, o_vg, vg_hbm, n).wait()


def local(NC, NT_, queries, keys, values, out_grad, gain, doc_ids):
    tok, W = queries.shape
    NB, NH = tok // C, W // HD
    PR = NH * HD // NC
    QW = W * NT_
    any_spec = pl.BlockSpec(memory_space=pl.ANY)
    vmem_spec = pl.BlockSpec(memory_space=pltpu.VMEM)
    out = jax.ShapeDtypeStruct((tok, W), BF16)
    dma = pltpu.SemaphoreType.DMA
    whole = pltpu.VMEM((NC, PR, HD), F32)
    part = pltpu.VMEM((NC // 2, PR, HD), F32)
    ring = [whole, part, part, whole, part, part, part]
    held = (
        pltpu.VMEM((tok, W), BF16),
        pltpu.VMEM((tok, W), BF16),
        pltpu.VMEM((tok, W), F32),
        pltpu.VMEM((tok, W), F32),
        pltpu.VMEM((NB, NH, HD, HD), BF16),
        pltpu.VMEM((tok, W), BF16),
        pltpu.VMEM((tok, W), BF16),
    )
    inner = pl.pallas_call(
        functools.partial(kernel, NC, NT_, NB, NH, QW),
        out_shape=held,
        in_specs=[pl.BlockSpec(memory_space=pltpu.SMEM)] + [any_spec] * 4 + [vmem_spec],
        out_specs=(vmem_spec,) * 7,
        scratch_shapes=[pltpu.VMEM((tok, W), BF16)] * 2
        + [
            pltpu.VMEM((NB * NH, C, C), BF16),
            pltpu.VMEM((tok, W), F32),
            pltpu.VMEM((tok, W), BF16),
            pltpu.VMEM((NB, NC, PR, HD), F32),
            pltpu.VMEM((NB, NH, HD, HD), BF16),
            pltpu.VMEM((NB, NC, PR, HD), F32),
        ]
        + [pltpu.VMEM((tok, HD), F32)] * 2
        + [pltpu.VMEM((2, 128), F32), pltpu.VMEM((NC, 2, 128), F32)]
        + ring
        + ring
        + [
            pltpu.VMEM((16, C), F32),
            pltpu.VMEM((NT_, 16, C), F32),
            dma((4, NB)),
            dma((NC,)),
            dma((NC,)),
            dma((NC // 2,)),
            dma((NC // 2,)),
            dma((NC // 2,)),
            dma((NC // 2,)),
            dma((4,)),
            dma((4,)),
            dma((NT_,)),
            dma((NT_,)),
        ],
        compiler_params=pltpu.CompilerParams(
            collective_id=0, has_side_effects=True, vmem_limit_bytes=47 * 2**20
        ),
        name="packed_linear_attention",
    )(doc_ids, queries, keys, values, out_grad, gain.reshape(1, W))
    return pl.pallas_call(
        functools.partial(finish, NB, NH),
        out_shape=(out,) * 4,
        in_specs=[vmem_spec] * 7,
        out_specs=(any_spec,) * 4,
        scratch_shapes=[pltpu.VMEM((tok, W), BF16)] * 2 + [dma((4, NB))],
        compiler_params=pltpu.CompilerParams(vmem_limit_bytes=8 * 2**20),
        name="key_value_grads",
    )(*inner)


def solution(mesh):
    ctx, tp = mesh.shape["ctx"], mesh.shape["tp"]
    return jax.shard_map(
        functools.partial(local, ctx, tp),
        mesh=mesh,
        in_specs=(
            P("ctx", "tp"),
            P("ctx", "tp"),
            P("ctx", "tp"),
            P("ctx", "tp"),
            P("tp"),
            P("ctx"),
        ),
        out_specs=(P("ctx", "tp"), P("ctx", "tp"), P("ctx", "tp"), P("ctx", "tp")),
        check_vma=False,
    )
```
